32 devices in a mesh: region: 16 (over z, y, core), freq: 2 (over x).
Axes of the slice: x: 2, y: 2, z: 4, core: 2. Of those that a mesh axis runs over, the one named last changes fastest.
Arguments:
- dirty_map: float32 [4, 16384], P('freq', 'region'), may hold values from -6 to 6
- psf_blocks: bfloat16 [4, 128, 7, 128, 128], P('freq', 'region'), as said below
- col_index: int32 [128, 7], P('region'), may hold values from 0 to 127, as said below
- block_live: int32 [128, 7], P('region'), may hold values from 0 to 1, as said below
Outputs:
- source_map: float32 [4, 16384], P('freq', 'region')
- broadband: float32 [16384], P('region')
The draws below stay inside these ranges and needn't reach their ends.
Inputs may be any that keep to these rules, and one draw needn't show every extreme that they name: `col_index`: block row i stores itself in slot 0; the pattern is symmetric: if row i names j then row j names i, and column offsets are the same for every row (mod 128). `block_live`: slot 0 is always 1; the flag of block (i, j) equals that of block (j, i). `psf_blocks`: the operator is symmetric: the block of row i naming column j is the transpose of the block of row j naming column i; diagonal entries of slot 0 lie between 0.9 and 1.1.
All inputs are finite; a program needn't handle non-finite values.
Results may differ from the reference program's by a relative error of at most 0.0032.
Values may be sent and summed in bfloat16 or wider, within the bound.
A program may use at most 64 MiB of HBM per device.

```python
import math
import jax
import jax.numpy as jnp
from jax import lax

BS = 128
K = 7
BR = 8
ITERS = 3
NBLK = 128
F = 4
G = 16384


def pattern(key):
    lowest = max(1, min(4 * BR, NBLK // 2 - 3))
    offsets = jax.random.permutation(jax.random.fold_in(key, 11), NBLK // 2 - lowest)[:(K - 1) // 2].astype(jnp.int32) + lowest
    indices = jnp.arange(NBLK, dtype=jnp.int32)[:, None]
    return jnp.concatenate([indices, (indices + offsets[None, :]) % NBLK, (indices - offsets[None, :]) % NBLK], axis=1).astype(jnp.int32)


def pair_codes(key):
    columns = pattern(key)
    owners = jnp.broadcast_to(jnp.arange(NBLK, dtype=jnp.int32)[:, None], columns.shape)
    lower = jnp.minimum(owners, columns)
    upper = jnp.maximum(owners, columns)
    return (columns, owners, lower, upper)


def draw_col_index(key, part):
    return pattern(key)


def draw_block_live(key, part):
    columns, owners, lower, upper = pair_codes(key)
    codes = (lower * NBLK + upper).reshape(-1)
    base_key = jax.random.fold_in(key, 23)
    hashes = jax.vmap(lambda code: jax.random.randint(jax.random.fold_in(base_key, code), (), 0, 100))(codes).reshape(lower.shape)
    region_count = NBLK // BR
    thresh = 85 + 15 * (upper // BR) // max(region_count - 1, 1)
    flags = (hashes < thresh).astype(jnp.int32)
    return jnp.where(lower == upper, 1, flags).astype(jnp.int32)


def draw_psf_blocks(key, part):
    columns, owners, lower, upper = pair_codes(key)
    codes = (lower * NBLK + upper).reshape(-1)
    above = (owners <= columns).reshape(-1)
    same = (lower == upper).reshape(-1)
    scale = 0.5 / math.sqrt(K * BS)
    base_key = jax.random.fold_in(key, 37)
    identity = jnp.eye(BS, dtype=jnp.float32)

    def one_block(freq_key, code, upper_side, on_diagonal):
        block_key = jax.random.fold_in(freq_key, code)
        raw = jnp.clip(jax.random.normal(block_key, (BS, BS), jnp.float32), -4.0, 4.0)
        flipped = jnp.where(upper_side, raw, raw.T) * scale
        centre = (raw + raw.T) * (0.70710678 * scale) * (1.0 - identity) + identity * (1.0 + 0.02 * raw)
        return jnp.where(on_diagonal, centre, flipped)

    def one_freq(index):
        freq_key = jax.random.fold_in(base_key, index)
        blocks = jax.vmap(one_block, in_axes=(None, 0, 0, 0))(freq_key, codes, above, same)
        return blocks.reshape(NBLK, K, BS, BS).astype(jnp.bfloat16)
    return lax.map(one_freq, jnp.arange(F, dtype=jnp.int32))


def steps_of(rng, extent, shards, low, high):
    def one(position, shards_of):
        draws = jax.random.uniform(jax.random.fold_in(jax.random.fold_in(rng, 6), position), (shards_of,), jnp.float32, low / len(shards), high / len(shards))
        return jnp.repeat(jnp.exp(draws), extent[position] // shards_of).reshape((-1,) + (1,) * (len(extent) - position - 1))

    level = one(*shards[0])
    for cut in shards[1:]:
        level = level * one(*cut)
    return level


def normal_values(stream_key, shape, width, most, shards=(), kind=jnp.bfloat16):
    loudness = steps_of(stream_key, shape, shards, -0.22, 0.18) if shards else 1.0
    drawn = jax.random.normal(stream_key, shape, jnp.float32) * width * loudness
    return jnp.minimum(jnp.maximum(drawn, -most), most).astype(kind)


def setup_inputs(seed: int = 0) -> dict:
    streams_of = jax.random.split(jax.random.key(seed), 5)
    return {
        "dirty_map": normal_values(streams_of[0], (F, G), 1.0, 6.0, ((0, 2), (1, 16)), jnp.float32),
        "psf_blocks": draw_psf_blocks(jax.random.fold_in(streams_of[4], 71), 0),
        "col_index": draw_col_index(jax.random.fold_in(streams_of[4], 71), 0),
        "block_live": draw_block_live(jax.random.fold_in(streams_of[4], 71), 0),
    }


def reference(dirty_map, psf_blocks, col_index, block_live):
    diagonal = jnp.diagonal(psf_blocks[:, :, 0], axis1=2, axis2=3).astype(jnp.float32).reshape(dirty_map.shape)
    alive_mask = block_live.astype(jnp.float32)
    source_map = jnp.maximum(0.0, dirty_map / diagonal)

    def apply_blocks(pair):
        blocks, values = pair
        spread = values.reshape(NBLK, BS).astype(jnp.float32)
        picked = spread[col_index] * alive_mask[:, :, None]
        applied = jnp.einsum("ikpq,ikq->ip", blocks.astype(jnp.float32), picked)
        return applied.reshape(-1)

    for iteration in range(ITERS):
        coarse = source_map.astype(jnp.bfloat16)
        applied = lax.map(apply_blocks, (psf_blocks, coarse))
        source_map = jnp.maximum(0.0, source_map + (dirty_map - applied) / diagonal)
    broadband = jnp.sum(source_map, axis=0)
    return source_map, broadband
```

```python
import functools

import jax
import jax.numpy as jnp
from jax import lax
from jax.experimental import pallas as pl
from jax.experimental.pallas import tpu as pltpu
from jax.sharding import PartitionSpec as P

ITERS = 3
MESH = pl.DeviceIdType.MESH
TRANSPOSED = (((1,), (1,)), ((), ()))


def kernel(
    regions,
    groups,
    dirty_ref,
    psf_hbm,
    col_ref,
    live_ref,
    est_ref,
    broad_ref,
    psf,
    target_ref,
    outgoing,
    arrived,
    spread,
    picked,
    partial,
    load_sem,
    send_sem,
    recv_sem,
    broad_send,
    broad_recv,
):
    me = lax.axis_index("region")
    group = lax.axis_index("freq")
    freq_count, row_blocks, slots, width = psf.shape[:4]
    rows = freq_count * row_blocks

    first = pltpu.make_async_copy(
        psf_hbm.at[:, :, pl.ds(0, 1)], psf.at[:, :, pl.ds(0, 1)], load_sem.at[0]
    )
    rest = pltpu.make_async_copy(
        psf_hbm.at[:, :, pl.ds(1, slots - 1)], psf.at[:, :, pl.ds(1, slots - 1)], load_sem.at[1]
    )
    first.start()
    rest.start()
    barrier = pltpu.get_barrier_semaphore()
    for step in range(1, regions):
        pl.semaphore_signal(
            barrier, inc=1, device_id={"region": lax.rem(me + step, regions)}, device_id_type=MESH
        )
    for step in range(1, groups):
        pl.semaphore_signal(
            barrier, inc=1, device_id={"freq": lax.rem(group + step, groups)}, device_id_type=MESH
        )

    for f in range(freq_count):
        for i in range(row_blocks):
            row = f * row_blocks + i
            target_ref[row : row + 1, :] = dirty_ref[f : f + 1, i * width : (i + 1) * width]
    target = target_ref[...]
    alive = [
        jnp.concatenate(
            [jnp.broadcast_to(live_ref[:, k : k + 1].astype(jnp.float32), (row_blocks, width))] * freq_count,
            axis=0,
        )
        for k in range(1, slots)
    ]
    alive = jnp.concatenate(alive, axis=1)
    row_ids = lax.broadcasted_iota(jnp.int32, (rows, width), 0)

    first.wait()
    eye = lax.broadcasted_iota(jnp.int32, (width, width), 0) == lax.broadcasted_iota(
        jnp.int32, (width, width), 1
    )
    diagonal = jnp.zeros((rows, width), jnp.float32)
    for f in range(freq_count):
        for i in range(row_blocks):
            block = psf[f, i, 0].astype(jnp.float32)
            line = jnp.sum(jnp.where(eye, block, 0.0), axis=0, keepdims=True)
            diagonal = jnp.where(row_ids == f * row_blocks + i, line, diagonal)
    estimate = jnp.maximum(0.0, target / diagonal)

    for iteration in range(ITERS):
        coarse = estimate.astype(jnp.bfloat16)
        outgoing[iteration] = coarse
        if iteration == 0:
            pl.semaphore_wait(barrier, regions - 1 + groups - 1)
        for step in range(1, regions):
            pltpu.make_async_remote_copy(
                src_ref=outgoing.at[iteration],
                dst_ref=arrived.at[iteration, me],
                send_sem=send_sem.at[iteration],
                recv_sem=recv_sem.at[iteration],
                device_id={"region": lax.rem(me + step, regions)},
                device_id_type=MESH,
            ).start()
        applied = jnp.zeros((rows, width), jnp.float32)
        for f in range(freq_count):
            for i in range(row_blocks):
                product = lax.dot_general(
                    coarse, psf[f, i, 0], TRANSPOSED, preferred_element_type=jnp.float32
                )
                applied = jnp.where(row_ids == f * row_blocks + i, product, applied)
        if iteration == 0:
            rest.wait()
        others = arrived.at[iteration, pl.ds(0, regions - 1)]
        pltpu.make_async_copy(others, others, recv_sem.at[iteration]).wait()
        arrived[iteration, me] = coarse
        spread[...] = arrived[iteration].astype(jnp.float32)
        for i in range(row_blocks):
            for k in range(1, slots):
                column = col_ref[i, k]
                owner = column // row_blocks
                inner = column % row_blocks
                for f in range(freq_count):
                    row = f * row_blocks + i
                    picked[row : row + 1, (k - 1) * width : k * width] = spread[
                        owner, pl.ds(f * row_blocks + inner, 1), :
                    ]
        chosen = (picked[...] * alive).astype(jnp.bfloat16)
        far = jnp.zeros((rows, width), jnp.float32)
        for f in range(freq_count):
            for i in range(row_blocks):
                blocks = jnp.concatenate([psf[f, i, k] for k in range(1, slots)], axis=1)
                product = lax.dot_general(
                    chosen, blocks, TRANSPOSED, preferred_element_type=jnp.float32
                )
                far = jnp.where(row_ids == f * row_blocks + i, product, far)
        estimate = jnp.maximum(0.0, estimate + (target - (applied + far)) / diagonal)

    local_sum = estimate[:row_blocks]
    for f in range(1, freq_count):
        local_sum = local_sum + estimate[f * row_blocks : (f + 1) * row_blocks]
    partial[group] = local_sum
    broad = []
    for step in range(1, groups):
        copy = pltpu.make_async_remote_copy(
            src_ref=partial.at[group],
            dst_ref=partial.at[group],
            send_sem=broad_send.at[step],
            recv_sem=broad_recv.at[step],
            device_id={"freq": lax.rem(group + step, groups)},
            device_id_type=MESH,
        )
        copy.start()
        broad.append(copy)
    est_ref[...] = estimate
    for iteration in range(ITERS):
        others = arrived.at[iteration, pl.ds(0, regions - 1)]
        pltpu.make_async_copy(others, others, send_sem.at[iteration]).wait()
    for copy in broad:
        copy.wait()
    total = partial[0]
    for g in range(1, groups):
        total = total + partial[g]
    broad_ref[...] = total


def solution(mesh):
    regions, groups = mesh.shape["region"], mesh.shape["freq"]

    def local(dirty_map, psf_blocks, col_index, block_live):
        freq_count, row_blocks, slots, width, _ = psf_blocks.shape
        rows = freq_count * row_blocks
        vmem = pl.BlockSpec(memory_space=pltpu.VMEM)
        estimate, broadband = pl.pallas_call(
            functools.partial(kernel, regions, groups),
            out_shape=(
                jax.ShapeDtypeStruct((rows, width), jnp.float32),
                jax.ShapeDtypeStruct((row_blocks, width), jnp.float32),
            ),
            in_specs=[
                vmem,
                pl.BlockSpec(memory_space=pl.ANY),
                pl.BlockSpec(memory_space=pltpu.SMEM),
                vmem,
            ],
            out_specs=(vmem, vmem),
            scratch_shapes=[
                pltpu.VMEM(psf_blocks.shape, jnp.bfloat16),
                pltpu.VMEM((rows, width), jnp.float32),
                pltpu.VMEM((ITERS, rows, width), jnp.bfloat16),
                pltpu.VMEM((ITERS, regions, rows, width), jnp.bfloat16),
                pltpu.VMEM((regions, rows, width), jnp.float32),
                pltpu.VMEM((rows, (slots - 1) * width), jnp.float32),
                pltpu.VMEM((groups, row_blocks, width), jnp.float32),
                pltpu.SemaphoreType.DMA((2,)),
                pltpu.SemaphoreType.DMA((ITERS,)),
                pltpu.SemaphoreType.DMA((ITERS,)),
                pltpu.SemaphoreType.DMA((groups,)),
                pltpu.SemaphoreType.DMA((groups,)),
            ],
            compiler_params=pltpu.CompilerParams(collective_id=0, has_side_effects=True),
        )(dirty_map, psf_blocks, col_index, block_live)
        return estimate.reshape(freq_count, row_blocks * width), broadband.reshape(-1)

    return jax.shard_map(
        local,
        mesh=mesh,
        in_specs=(
            P("freq", "region"),
            P("freq", "region", None, None, None),
            P("region", None),
            P("region", None),
        ),
        out_specs=(P("freq", "region"), P("region")),
        check_vma=False,
    )
```

```python
import functools

import jax
import jax.numpy as jnp
from jax import lax
from jax.experimental import pallas as pl
from jax.experimental.pallas import tpu as pltpu
from jax.sharding import PartitionSpec as P

ITERS = 3
MESH = pl.DeviceIdType.MESH


def kernel(
    regions,
    groups,
    dirty_hbm,
    psf_hbm,
    col_hbm,
    live_hbm,
    est_ref,
    broad_ref,
    psf,
    turned,
    dirty_ref,
    col_ref,
    live_ref,
    target_ref,
    outgoing,
    arrived,
    spread,
    picked,
    partial,
    load_sem,
    send_sem,
    recv_sem,
    broad_send,
    broad_recv,
):
    me = lax.axis_index("region")
    group = lax.axis_index("freq")
    freq_count, row_blocks, slots, width = psf.shape[:4]
    rows = freq_count * row_blocks

    barrier = pltpu.get_barrier_semaphore()
    for step in range(1, regions):
        pl.semaphore_signal(
            barrier, inc=1, device_id={"region": lax.rem(me + step, regions)}, device_id_type=MESH
        )
    for step in range(1, groups):
        pl.semaphore_signal(
            barrier, inc=1, device_id={"freq": lax.rem(group + step, groups)}, device_id_type=MESH
        )

    first = pltpu.make_async_copy(
        psf_hbm.at[:, :, pl.ds(0, 1)], psf.at[:, :, pl.ds(0, 1)], load_sem.at[0]
    )
    rest = pltpu.make_async_copy(
        psf_hbm.at[:, :, pl.ds(1, slots - 1)], psf.at[:, :, pl.ds(1, slots - 1)], load_sem.at[1]
    )
    first.start()
    small = [
        pltpu.make_async_copy(source, target, load_sem.at[2 + n])
        for n, (source, target) in enumerate(
            ((dirty_hbm, dirty_ref), (live_hbm, live_ref), (col_hbm, col_ref))
        )
    ]
    for copy in small:
        copy.start()
    rest.start()

    for copy in small:
        copy.wait()
    for f in range(freq_count):
        for i in range(row_blocks):
            row = f * row_blocks + i
            target_ref[row : row + 1, :] = dirty_ref[f : f + 1, i * width : (i + 1) * width]
    target = target_ref[...]
    alive = [
        jnp.concatenate(
            [jnp.broadcast_to(live_ref[:, k : k + 1].astype(jnp.float32), (row_blocks, width))] * freq_count,
            axis=0,
        )
        for k in range(1, slots)
    ]
    alive = jnp.concatenate(alive, axis=1)
    row_ids = lax.broadcasted_iota(jnp.int32, (rows, width), 0)

    first.wait()
    eye = lax.broadcasted_iota(jnp.int32, (width, width), 0) == lax.broadcasted_iota(
        jnp.int32, (width, width), 1
    )
    diagonal = jnp.zeros((rows, width), jnp.float32)
    for f in range(freq_count):
        for i in range(row_blocks):
            block = psf[f, i, 0].astype(jnp.float32)
            line = jnp.sum(jnp.where(eye, block, 0.0), axis=0, keepdims=True)
            diagonal = jnp.where(row_ids == f * row_blocks + i, line, diagonal)
    estimate = jnp.maximum(0.0, target / diagonal)

    for iteration in range(ITERS):
        coarse = estimate.astype(jnp.bfloat16)
        outgoing[iteration] = coarse
        if iteration == 0:
            pl.semaphore_wait(barrier, regions - 1 + groups - 1)
        for step in range(1, regions):
            pltpu.make_async_remote_copy(
                src_ref=outgoing.at[iteration],
                dst_ref=arrived.at[iteration, me],
                send_sem=send_sem.at[iteration],
                recv_sem=recv_sem.at[iteration],
                device_id={"region": lax.rem(me + step, regions)},
                device_id_type=MESH,
            ).start()
        if iteration == 0:
            rest.wait()
            for f in range(freq_count):
                for i in range(row_blocks):
                    for k in range(1, slots):
                        turned[f, i, (k - 1) * width : k * width, :] = psf[f, i, k].T
        applied = jnp.zeros((rows, width), jnp.float32)
        for f in range(freq_count):
            for i in range(row_blocks):
                product = jnp.dot(coarse, psf[f, i, 0], preferred_element_type=jnp.float32)
                applied = jnp.where(row_ids == f * row_blocks + i, product, applied)
        others = arrived.at[iteration, pl.ds(0, regions - 1)]
        pltpu.make_async_copy(others, others, recv_sem.at[iteration]).wait()
        arrived[iteration, me] = coarse
        spread[...] = arrived[iteration].astype(jnp.float32)
        for i in range(row_blocks):
            for k in range(1, slots):
                column = col_ref[i, k]
                owner = column // row_blocks
                inner = column % row_blocks
                for f in range(freq_count):
                    row = f * row_blocks + i
                    picked[row : row + 1, (k - 1) * width : k * width] = spread[
                        owner, pl.ds(f * row_blocks + inner, 1), :
                    ]
        chosen = (picked[...] * alive).astype(jnp.bfloat16)
        far = jnp.zeros((rows, width), jnp.float32)
        for f in range(freq_count):
            for i in range(row_blocks):
                product = jnp.dot(chosen, turned[f, i], preferred_element_type=jnp.float32)
                far = jnp.where(row_ids == f * row_blocks + i, product, far)
        estimate = jnp.maximum(0.0, estimate + (target - (applied + far)) / diagonal)

    local_sum = estimate[:row_blocks]
    for f in range(1, freq_count):
        local_sum = local_sum + estimate[f * row_blocks : (f + 1) * row_blocks]
    partial[group] = local_sum
    broad = []
    for step in range(1, groups):
        copy = pltpu.make_async_remote_copy(
            src_ref=partial.at[group],
            dst_ref=partial.at[group],
            send_sem=broad_send.at[step],
            recv_sem=broad_recv.at[step],
            device_id={"freq": lax.rem(group + step, groups)},
            device_id_type=MESH,
        )
        copy.start()
        broad.append(copy)
    for f in range(freq_count):
        for i in range(row_blocks):
            row = f * row_blocks + i
            est_ref[f : f + 1, i * width : (i + 1) * width] = estimate[row : row + 1]
    for iteration in range(ITERS):
        others = arrived.at[iteration, pl.ds(0, regions - 1)]
        pltpu.make_async_copy(others, others, send_sem.at[iteration]).wait()
    for copy in broad:
        copy.wait()
    total = partial[0]
    for g in range(1, groups):
        total = total + partial[g]
    broad_ref[...] = total


def write_out(est_ref, broad_ref, est_out, broad_out, sems):
    copies = [
        pltpu.make_async_copy(est_ref, est_out, sems.at[0]),
        pltpu.make_async_copy(broad_ref, broad_out, sems.at[1]),
    ]
    for copy in copies:
        copy.start()
    for copy in copies:
        copy.wait()


def solution(mesh):
    regions, groups = mesh.shape["region"], mesh.shape["freq"]

    def local(dirty_map, psf_blocks, col_index, block_live):
        freq_count, row_blocks, slots, width, _ = psf_blocks.shape
        rows = freq_count * row_blocks
        vmem = pl.BlockSpec(memory_space=pltpu.VMEM)
        anywhere = pl.BlockSpec(memory_space=pl.ANY)
        estimate, broadband = pl.pallas_call(
            functools.partial(kernel, regions, groups),
            out_shape=(pltpu.VMEM(dirty_map.shape, jnp.float32), pltpu.VMEM((row_blocks, width), jnp.float32)),
            in_specs=[anywhere] * 4,
            out_specs=(vmem, vmem),
            scratch_shapes=[
                pltpu.VMEM(psf_blocks.shape, jnp.bfloat16),
                pltpu.VMEM((freq_count, row_blocks, (slots - 1) * width, width), jnp.bfloat16),
                pltpu.VMEM(dirty_map.shape, jnp.float32),
                pltpu.SMEM(col_index.shape, jnp.int32),
                pltpu.VMEM(block_live.shape, jnp.int32),
                pltpu.VMEM((rows, width), jnp.float32),
                pltpu.VMEM((ITERS, rows, width), jnp.bfloat16),
                pltpu.VMEM((ITERS, regions, rows, width), jnp.bfloat16),
                pltpu.VMEM((regions, rows, width), jnp.float32),
                pltpu.VMEM((rows, (slots - 1) * width), jnp.float32),
                pltpu.VMEM((groups, row_blocks, width), jnp.float32),
                pltpu.SemaphoreType.DMA((5,)),
                pltpu.SemaphoreType.DMA((ITERS,)),
                pltpu.SemaphoreType.DMA((ITERS,)),
                pltpu.SemaphoreType.DMA((groups,)),
                pltpu.SemaphoreType.DMA((groups,)),
            ],
            compiler_params=pltpu.CompilerParams(collective_id=0, has_side_effects=True),
        )(dirty_map, psf_blocks, col_index, block_live)
        estimate, broadband = pl.pallas_call(
            write_out,
            out_shape=(
                jax.ShapeDtypeStruct(dirty_map.shape, jnp.float32),
                jax.ShapeDtypeStruct((row_blocks, width), jnp.float32),
            ),
            in_specs=[vmem, vmem],
            out_specs=(anywhere, anywhere),
            scratch_shapes=[pltpu.SemaphoreType.DMA((2,))],
        )(
            pltpu.with_memory_space_constraint(estimate, pltpu.VMEM),
            pltpu.with_memory_space_constraint(broadband, pltpu.VMEM),
        )
        return estimate, broadband.reshape(-1)

    return jax.shard_map(
        local,
        mesh=mesh,
        in_specs=(
            P("freq", "region"),
            P("freq", "region", None, None, None),
            P("region", None),
            P("region", None),
        ),
        out_specs=(P("freq", "region"), P("region")),
        check_vma=False,
    )
```

```python
import functools

import jax
import jax.numpy as jnp
from jax import lax
from jax.experimental import pallas as pl
from jax.experimental.pallas import tpu as pltpu
from jax.sharding import PartitionSpec as P

ITERS = 3
MESH = pl.DeviceIdType.MESH


def partners(me, regions):
    if regions & (regions - 1):
        return [lax.rem(me + step, regions) for step in range(1, regions)]
    moves, bit = [], 1
    while bit < regions:
        moves.append(bit - 2 * bit * ((me // bit) % 2))
        bit *= 2
    return [
        sum((move for n, move in enumerate(moves) if mask >> n & 1), me)
        for mask in range(regions - 1, 0, -1)
    ]


def kernel(
    regions,
    groups,
    dirty_hbm,
    psf_hbm,
    col_hbm,
    live_hbm,
    est_ref,
    broad_ref,
    psf,
    turned,
    dirty_ref,
    col_ref,
    live_ref,
    target_ref,
    outgoing,
    arrived,
    spread,
    picked,
    partial,
    load_sem,
    send_sem,
    recv_sem,
    broad_send,
    broad_recv,
):
    me = lax.axis_index("region")
    group = lax.axis_index("freq")
    peers = partners(me, regions)
    freq_count, row_blocks, slots, width = psf.shape[:4]
    rows = freq_count * row_blocks

    first = pltpu.make_async_copy(
        psf_hbm.at[:, :, pl.ds(0, 1)], psf.at[:, :, pl.ds(0, 1)], load_sem.at[0]
    )
    first.start()
    barrier = pltpu.get_barrier_semaphore()
    for peer in peers:
        pl.semaphore_signal(
            barrier, inc=1, device_id={"region": peer}, device_id_type=MESH
        )
    for step in range(1, groups):
        pl.semaphore_signal(
            barrier, inc=1, device_id={"freq": lax.rem(group + step, groups)}, device_id_type=MESH
        )

    rest = pltpu.make_async_copy(
        psf_hbm.at[:, :, pl.ds(1, slots - 1)], psf.at[:, :, pl.ds(1, slots - 1)], load_sem.at[1]
    )
    small = [
        pltpu.make_async_copy(source, target, load_sem.at[2 + n])
        for n, (source, target) in enumerate(
            ((dirty_hbm, dirty_ref), (live_hbm, live_ref), (col_hbm, col_ref))
        )
    ]
    for copy in small:
        copy.start()
    rest.start()

    for copy in small:
        copy.wait()
    for f in range(freq_count):
        for i in range(row_blocks):
            row = f * row_blocks + i
            target_ref[row : row + 1, :] = dirty_ref[f : f + 1, i * width : (i + 1) * width]
    target = target_ref[...]
    alive = [
        jnp.concatenate(
            [jnp.broadcast_to(live_ref[:, k : k + 1].astype(jnp.float32), (row_blocks, width))] * freq_count,
            axis=0,
        )
        for k in range(1, slots)
    ]
    alive = jnp.concatenate(alive, axis=1)
    row_ids = lax.broadcasted_iota(jnp.int32, (rows, width), 0)

    first.wait()
    eye = lax.broadcasted_iota(jnp.int32, (width, width), 0) == lax.broadcasted_iota(
        jnp.int32, (width, width), 1
    )
    diagonal = jnp.zeros((rows, width), jnp.float32)
    for f in range(freq_count):
        for i in range(row_blocks):
            block = psf[f, i, 0].astype(jnp.float32)
            line = jnp.sum(jnp.where(eye, block, 0.0), axis=0, keepdims=True)
            diagonal = jnp.where(row_ids == f * row_blocks + i, line, diagonal)
    estimate = jnp.maximum(0.0, target / diagonal)

    def send(iteration):
        for peer in peers:
            pltpu.make_async_remote_copy(
                src_ref=outgoing.at[iteration],
                dst_ref=arrived.at[iteration, me],
                send_sem=send_sem.at[iteration],
                recv_sem=recv_sem.at[iteration],
                device_id={"region": peer},
                device_id_type=MESH,
            ).start()

    outgoing[0] = estimate.astype(jnp.bfloat16)
    pl.semaphore_wait(barrier, regions - 1 + groups - 1)
    send(0)
    rest.wait()
    def turn(row, carry):
        f, i = row // row_blocks, row % row_blocks
        for k in range(1, slots):
            turned[f, i, (k - 1) * width : k * width, :] = psf[f, i, k].T
        return carry

    lax.fori_loop(0, rows, turn, 0)
    def sweep(iteration, estimate):
        coarse = estimate.astype(jnp.bfloat16)
        applied = jnp.zeros((rows, width), jnp.float32)
        for f in range(freq_count):
            for i in range(row_blocks):
                product = jnp.dot(coarse, psf[f, i, 0], preferred_element_type=jnp.float32)
                applied = jnp.where(row_ids == f * row_blocks + i, product, applied)
        others = arrived.at[iteration, pl.ds(0, regions - 1)]
        pltpu.make_async_copy(others, others, recv_sem.at[iteration]).wait()
        arrived[iteration, me] = coarse
        spread[...] = arrived[iteration].astype(jnp.float32)
        for i in range(row_blocks):
            for k in range(1, slots):
                column = col_ref[i, k]
                owner = column // row_blocks
                inner = column % row_blocks
                for f in range(freq_count):
                    row = f * row_blocks + i
                    picked[row : row + 1, (k - 1) * width : k * width] = spread[
                        owner, pl.ds(f * row_blocks + inner, 1), :
                    ]
        chosen = (picked[...] * alive).astype(jnp.bfloat16)
        far = jnp.zeros((rows, width), jnp.float32)
        for f in range(freq_count):
            for i in range(0, row_blocks, 2):
                blocks = jnp.concatenate([turned[f, i], turned[f, i + 1]], axis=1)
                product = jnp.dot(chosen, blocks, preferred_element_type=jnp.float32)
                for j in range(2):
                    part = product[:, j * width : (j + 1) * width]
                    far = jnp.where(row_ids == f * row_blocks + i + j, part, far)
        estimate = jnp.maximum(0.0, estimate + (target - (applied + far)) / diagonal)

        @pl.when(iteration < ITERS - 1)
        def _():
            outgoing[iteration + 1] = estimate.astype(jnp.bfloat16)
            send(iteration + 1)

        return estimate

    estimate = lax.fori_loop(0, ITERS, sweep, estimate)
    local_sum = estimate[:row_blocks]
    for f in range(1, freq_count):
        local_sum = local_sum + estimate[f * row_blocks : (f + 1) * row_blocks]
    partial[group] = local_sum
    broad = []
    for step in range(1, groups):
        copy = pltpu.make_async_remote_copy(
            src_ref=partial.at[group],
            dst_ref=partial.at[group],
            send_sem=broad_send.at[step],
            recv_sem=broad_recv.at[step],
            device_id={"freq": lax.rem(group + step, groups)},
            device_id_type=MESH,
        )
        copy.start()
        broad.append(copy)
    for f in range(freq_count):
        for i in range(row_blocks):
            row = f * row_blocks + i
            est_ref[f : f + 1, i * width : (i + 1) * width] = estimate[row : row + 1]
    for iteration in range(ITERS):
        others = arrived.at[iteration, pl.ds(0, regions - 1)]
        pltpu.make_async_copy(others, others, send_sem.at[iteration]).wait()
    for copy in broad:
        copy.wait()
    total = partial[0]
    for g in range(1, groups):
        total = total + partial[g]
    broad_ref[...] = total


def write_out(est_ref, broad_ref, est_out, broad_out, sems):
    copies = [
        pltpu.make_async_copy(est_ref, est_out, sems.at[0]),
        pltpu.make_async_copy(broad_ref, broad_out, sems.at[1]),
    ]
    for copy in copies:
        copy.start()
    for copy in copies:
        copy.wait()


def solution(mesh):
    regions, groups = mesh.shape["region"], mesh.shape["freq"]

    def local(dirty_map, psf_blocks, col_index, block_live):
        freq_count, row_blocks, slots, width, _ = psf_blocks.shape
        rows = freq_count * row_blocks
        vmem = pl.BlockSpec(memory_space=pltpu.VMEM)
        anywhere = pl.BlockSpec(memory_space=pl.ANY)
        estimate, broadband = pl.pallas_call(
            functools.partial(kernel, regions, groups),
            out_shape=(pltpu.VMEM(dirty_map.shape, jnp.float32), pltpu.VMEM((row_blocks, width), jnp.float32)),
            in_specs=[anywhere] * 4,
            out_specs=(vmem, vmem),
            scratch_shapes=[
                pltpu.VMEM(psf_blocks.shape, jnp.bfloat16),
                pltpu.VMEM((freq_count, row_blocks, (slots - 1) * width, width), jnp.bfloat16),
                pltpu.VMEM(dirty_map.shape, jnp.float32),
                pltpu.SMEM(col_index.shape, jnp.int32),
                pltpu.VMEM(block_live.shape, jnp.int32),
                pltpu.VMEM((rows, width), jnp.float32),
                pltpu.VMEM((ITERS, rows, width), jnp.bfloat16),
                pltpu.VMEM((ITERS, regions, rows, width), jnp.bfloat16),
                pltpu.VMEM((regions, rows, width), jnp.float32),
                pltpu.VMEM((rows, (slots - 1) * width), jnp.float32),
                pltpu.VMEM((groups, row_blocks, width), jnp.float32),
                pltpu.SemaphoreType.DMA((5,)),
                pltpu.SemaphoreType.DMA((ITERS,)),
                pltpu.SemaphoreType.DMA((ITERS,)),
                pltpu.SemaphoreType.DMA((groups,)),
                pltpu.SemaphoreType.DMA((groups,)),
            ],
            compiler_params=pltpu.CompilerParams(collective_id=0, has_side_effects=True),
        )(dirty_map, psf_blocks, col_index, block_live)
        estimate, broadband = pl.pallas_call(
            write_out,
            out_shape=(
                jax.ShapeDtypeStruct(dirty_map.shape, jnp.float32),
                jax.ShapeDtypeStruct((row_blocks, width), jnp.float32),
            ),
            in_specs=[vmem, vmem],
            out_specs=(anywhere, anywhere),
            scratch_shapes=[pltpu.SemaphoreType.DMA((2,))],
        )(
            pltpu.with_memory_space_constraint(estimate, pltpu.VMEM),
            pltpu.with_memory_space_constraint(broadband, pltpu.VMEM),
        )
        return estimate, broadband.reshape(-1)

    return jax.shard_map(
        local,
        mesh=mesh,
        in_specs=(
            P("freq", "region"),
            P("freq", "region", None, None, None),
            P("region", None),
            P("region", None),
        ),
        out_specs=(P("freq", "region"), P("region")),
        check_vma=False,
    )
```
